32 devices in a mesh: rows: 8 (over z, y), sub: 4 (over x, core).
Axes of the slice: x: 2, y: 2, z: 4, core: 2. Of those that a mesh axis runs over, the one named last changes fastest.
Arguments:
- embeddings: bfloat16 [16384, 768], P(('rows', 'sub')), may hold values from -0.25 to 0.25
- factor: float32 [16384, 512], P(('rows', 'sub')), may hold values from -0.15 to 0.15
- diagonal: float32 [16384], P(('rows', 'sub')), may hold values from 0.5 to 1
- pivot_owner: int32 [4, 256], replicated, may hold values from 0 to 31, as said below
- pivot_local: int32 [4, 256], replicated, may hold values from 0 to 511, as said below
Outputs:
- new_columns: float32 [16384, 1024], P(('rows', 'sub'))
- new_diagonal: float32 [16384], P(('rows', 'sub'))
The draws below stay inside these ranges and needn't reach their ends.
Inputs may be any that keep to these rules, and one draw needn't show every extreme that they name: The 1024 global rows pivot_owner * 512 + pivot_local are all different; row 0 and the last row of all are among them. `pivot_local`: read together with pivot_owner.
All inputs are finite; a program needn't handle non-finite values.
Results may differ from the reference program's by a relative error of at most 0.0003.
Values sent between devices are 32-bit elements; how exact they have to be, the bound alone decides.
No kernel may reach another device: no remote copies, remote signals or barrier semaphores. Data moves between devices by JAX's collectives and lax.ppermute only.
A program may use at most 64 MiB of HBM per device.

```python
import jax
import jax.numpy as jnp
from jax import lax

D = 768
K = 256
BLOCKS = 4
R0 = 512
ROWS_DEV = 512
N = 16384


def pivot_rows_drawn(key):
    inner = jax.random.permutation(jax.random.fold_in(key, 17), N - 2)[:BLOCKS * K] + 1
    chosen = inner.reshape(BLOCKS, K).astype(jnp.int32)
    chosen = chosen.at[0, 0].set(N - 1)
    chosen = chosen.at[BLOCKS - 1, 0].set(0)
    return chosen


def draw_pivot_owner(key, part):
    return (pivot_rows_drawn(key) // ROWS_DEV).astype(jnp.int32)


def draw_pivot_local(key, part):
    return (pivot_rows_drawn(key) % ROWS_DEV).astype(jnp.int32)


def steps_of(stream_key, shape, cuts, smallest, largest):
    loudness = 1.0
    for position, blocks in cuts:
        steps = jax.random.uniform(jax.random.fold_in(jax.random.fold_in(stream_key, 6), position), (blocks,), jnp.float32, smallest / len(cuts), largest / len(cuts))
        loudness = loudness * jnp.repeat(jnp.exp(steps), shape[position] // blocks).reshape((-1,) + (1,) * (len(shape) - 1 - position))
    return loudness


def noise(rng, dims, deviation, bound, shards=(), kind=jnp.bfloat16):
    entries = deviation * jax.random.normal(rng, dims, jnp.float32)
    if shards:
        entries = entries * steps_of(rng, dims, shards, -0.22, 0.18)
    return jnp.clip(entries, -bound, bound).astype(kind)


def setup_inputs(seed: int = 0) -> dict:
    key_of = jax.random.split(jax.random.key(seed), 6)
    return {
        "embeddings": noise(key_of[0], (N, D), 0.036, 0.25, ((0, 32),)),
        "factor": noise(key_of[1], (N, R0), 0.02, 0.15, ((0, 32),), jnp.float32),
        "diagonal": jnp.clip(0.5 + 0.5 * jax.random.uniform(key_of[2], (N,), jnp.float32) ** steps_of(key_of[2], (N,), ((0, 32),), -0.2, 0.2), 0.5, 1.0),
        "pivot_owner": draw_pivot_owner(jax.random.fold_in(key_of[5], 71), 0),
        "pivot_local": draw_pivot_local(jax.random.fold_in(key_of[5], 71), 0),
    }


gamma_scale = 1.0
ridge_base = 0.5

def gauss_kernel(left, left_squares, right, right_squares):
    inner = jnp.dot(left.astype(jnp.float32), right.T.astype(jnp.float32), preferred_element_type=jnp.float32)
    return jnp.exp(-gamma_scale * (left_squares[:, None] + right_squares[None, :] - 2.0 * inner))

def gershgorin(pivot_gram):
    absolute = jnp.sum(jnp.abs(pivot_gram), axis=1) - jnp.abs(jnp.diagonal(pivot_gram))
    return ridge_base + jnp.maximum(jnp.max(absolute - jnp.diagonal(pivot_gram)), 0.0)

def reference(embeddings, factor, diagonal, pivot_owner, pivot_local):
    squares = jnp.sum(jnp.square(embeddings.astype(jnp.float32)), axis=1)
    columns = factor
    residual_diag = diagonal
    blocks_out = []
    for block in range(BLOCKS):
        chosen = (pivot_owner[block] * ROWS_DEV + pivot_local[block]).astype(jnp.int32)
        points = jnp.take(embeddings, chosen, axis=0)
        point_squares = jnp.take(squares, chosen, axis=0)
        factor_rows = jnp.take(columns, chosen, axis=0)
        kernel = gauss_kernel(embeddings, squares, points, point_squares)
        resid = kernel - jnp.dot(columns, factor_rows.T, precision=lax.Precision.HIGHEST)
        pivot_kernel = gauss_kernel(points, point_squares, points, point_squares)
        pivot_gram = pivot_kernel - jnp.dot(factor_rows, factor_rows.T, precision=lax.Precision.HIGHEST)
        pivot_gram = 0.5 * (pivot_gram + pivot_gram.T)
        shift = gershgorin(pivot_gram)
        lower = jnp.linalg.cholesky(pivot_gram + shift * jnp.eye(K, dtype=jnp.float32))
        solved = lax.linalg.triangular_solve(lower, resid.T, left_side=True, lower=True)
        block_cols = solved.T
        residual_diag = residual_diag - jnp.sum(block_cols * block_cols, axis=1)
        columns = jnp.concatenate([columns, block_cols], axis=1)
        blocks_out.append(block_cols)
    return (jnp.concatenate(blocks_out, axis=1), residual_diag)
```

```python
import functools

import jax
import jax.numpy as jnp
from jax import lax
from jax.experimental import pallas as pl
from jax.experimental.pallas import tpu as pltpu
from jax.sharding import PartitionSpec as P

gamma_scale = 1.0
ridge_base = 0.5
AXES = ("rows", "sub")
F32 = jnp.float32
BF16 = jnp.bfloat16
VMEM_LIMIT = 60 * 1024 * 1024
TOL2 = 0.03 * 0.03
MAX_NEWTON = 12


def nt(a, b):
    return lax.dot_general(a, b, (((1,), (1,)), ((), ())), preferred_element_type=F32)


def nn(a, b):
    return lax.dot_general(a, b, (((1,), (0,)), ((), ())), preferred_element_type=F32)


def split(a):
    high = a.astype(BF16)
    return high, (a - high.astype(F32)).astype(BF16)


def nt3(a, b):
    return nt(a[0], b[0]) + (nt(a[0], b[1]) + nt(a[1], b[0]))


def nn3(a, b):
    return nn(a[0], b[0]) + (nn(a[0], b[1]) + nn(a[1], b[0]))


def plan(n, pivots):
    mean = pivots / n
    tiles = max(1, -int(-(mean + 4.25 * mean**0.5) // 8))
    bits = n.bit_length() - 1
    base = list(range(bits - 1, 0, -1))
    orders = [base]
    if len(base) > 2:
        orders += [
            base[-1:] + base[:-1],
            base[-2:-1] + base[:-2] + base[-1:],
            base[:-2] + base[-1:] + base[-2:-1],
        ]
    count = min(len(orders), tiles)
    sizes = [8 * (tiles // count + (1 if p < tiles % count else 0)) for p in range(count)]
    return sizes, orders[:count]


def select_kernel(sizes, me_ref, owner_ref, local_ref, emb_ref, fac_ref, *out_refs):
    me = me_ref[0]
    blocks, pivots = owner_ref.shape
    rows, width = emb_ref.shape
    cap = sum(sizes)
    padded = -(-cap // 16) * 16
    before = lax.broadcasted_iota(jnp.int32, (pivots, pivots), 0) < lax.broadcasted_iota(
        jnp.int32, (pivots, pivots), 1
    )
    before = jnp.where(before, 1.0, 0.0).astype(BF16)
    mine = jnp.where(owner_ref[...] == me, 1.0, 0.0)
    prefix = nn(mine.astype(BF16), before)
    totals = jnp.sum(mine, axis=1, keepdims=True)
    slots = lax.broadcasted_iota(jnp.int32, (padded, 1), 0).astype(F32)
    where = jnp.zeros((padded, 1), F32)
    offset = jnp.zeros((1, 1), F32)
    for b in range(blocks):
        slot = prefix[b : b + 1] + offset
        hit = (slot == slots) & (mine[b : b + 1] > 0.0)
        where += jnp.sum(
            jnp.where(hit, local_ref[b : b + 1, :].astype(F32), 0.0), axis=1, keepdims=True
        )
        offset = offset + totals[b : b + 1]
    positions = lax.broadcasted_iota(jnp.int32, (padded, rows), 1).astype(F32)
    onehot = jnp.where(where == positions, 1.0, 0.0).astype(BF16)
    points = nn(onehot, emb_ref[...])
    factor = fac_ref[...]
    high, rest = split(factor)
    rest = factor - high.astype(F32)
    middle, low = split(rest)
    picked = nn(onehot, high) + nn(onehot, middle) + nn(onehot, low)
    start = 0
    for size, out_ref in zip(sizes, out_refs, strict=True):
        out_ref[:, :width] = points[start : start + size]
        out_ref[:, width:] = picked[start : start + size]
        start += size


def main_kernel(
    width,
    blocks,
    idx_ref,
    emb_ref,
    fac_ref,
    diag_ref,
    *refs,
):
    nbuf = len(refs) - 2 - 9
    buf_refs = refs[:nbuf]
    out_ref, newdiag_ref = refs[nbuf : nbuf + 2]
    stage, gathered, e_ref, fh_ref, fl_ref, sq_ref, rg, w_ref, sem = refs[nbuf + 2 :]
    local = emb_ref.shape[0]
    total = idx_ref.shape[0]
    k = total // blocks
    copies = []
    start = 0
    for i, buf in enumerate(buf_refs):
        copies.append(
            pltpu.make_async_copy(buf, stage.at[pl.ds(start, buf.shape[0]), :], sem.at[i])
        )
        start += buf.shape[0]
    for copy in copies:
        copy.start()
    e_ref[total:, :] = emb_ref[...]
    high, low = split(fac_ref[...])
    fh_ref[total:, :] = high
    fl_ref[total:, :] = low
    wide = emb_ref[...].astype(F32)
    sq_ref[total:, :] = jnp.sum(wide * wide, axis=1, keepdims=True)
    for copy in copies:
        copy.wait()

    def gather(g, carry):
        for j in range(8):
            gathered[pl.ds(g * 8 + j, 1), :] = stage[pl.ds(idx_ref[g * 8 + j], 1), :]
        return carry

    lax.fori_loop(0, total // 8, gather, 0)
    ones = jnp.ones((8, width), BF16)
    row_squares = []
    for b in range(blocks):
        rows = pl.ds(b * k, k)
        wide = gathered[rows, :width]
        e_ref[rows, :] = wide.astype(BF16)
        high, low = split(gathered[rows, width:])
        fh_ref[rows, :] = high
        fl_ref[rows, :] = low
        square = wide * wide
        sq_ref[rows, :] = jnp.sum(square, axis=1, keepdims=True)
        high, low = split(square)
        row_squares.append((nt(ones, high) + nt(ones, low))[:1])
    for b in range(blocks):
        cols = pl.ds(b * k, k)
        eb, fb = e_ref[cols, :], (fh_ref[cols, :], fl_ref[cols, :])
        row_square = row_squares[b]

        def tile(t, carry, b=b, eb=eb, fb=fb, row_square=row_square):
            rows = pl.ds(pl.multiple_of(t * k, k), k)
            inner = nt(e_ref[rows, :], eb)
            kernel = jnp.exp(-gamma_scale * (sq_ref[rows, :] + row_square - 2.0 * inner))
            rg[rows, b * k : (b + 1) * k] = kernel - nt3((fh_ref[rows, :], fl_ref[rows, :]), fb)
            return carry

        lax.fori_loop(b, (total + local) // k, tile, 0)

    row = lax.broadcasted_iota(jnp.int32, (k, k), 0)
    col = lax.broadcasted_iota(jnp.int32, (k, k), 1)
    identity = jnp.where(row == col, 1.0, 0.0)
    lower = jnp.where(row > col, 1.0, 0.0) + 0.5 * identity
    new_diag = diag_ref[...]
    for b in range(blocks):
        gram = rg[b * k : (b + 1) * k, b * k : (b + 1) * k]
        diag = jnp.sum(gram * identity, axis=0, keepdims=True)
        off = jnp.sum(jnp.abs(gram), axis=0, keepdims=True) - jnp.abs(diag)
        shift = ridge_base + jnp.maximum(jnp.max(off - diag, axis=1, keepdims=True), 0.0)
        scale = shift + jnp.max(diag, axis=1, keepdims=True)
        shifted = (gram + shift * identity) / scale
        sh, sl = split(shifted)

        def update(error):
            f = error * lower
            fb = f.astype(BF16)
            return f - nn(fb, fb) - nt(fb, fb) * lower

        w = identity - update(shifted - identity)
        wb = w.astype(BF16)
        step = update(nt(nn(wb, sh).astype(BF16), wb) - identity)
        w = w - nn(step.astype(BF16), wb)

        def newton(w):
            ws = split(w)
            error = nt3(split(nn3(ws, (sh, sl))), ws) - identity
            w = w - nn3(split(update(error)), ws)
            return w, jnp.sum(error * error)

        w, norm = newton(w)
        w_ref[...] = w

        def more(state):
            i, norm = state
            return jnp.logical_and(i < MAX_NEWTON, jnp.logical_not(norm < TOL2))

        def again(state):
            i, norm = state
            w, norm = newton(w_ref[...])
            w_ref[...] = w
            return i + 1, norm

        _, norm = lax.while_loop(more, again, (0, norm))

        @pl.when(jnp.logical_not(norm < TOL2))
        def _():
            rg[b * k : (b + 1) * k, b * k : (b + 1) * k] = shifted
            w_ref[...] = identity

            def eliminate(j, carry):
                pivot_row = rg[pl.ds(b * k + j, 1), b * k : (b + 1) * k]
                unit_row = w_ref[pl.ds(j, 1), :]
                at = lax.broadcasted_iota(jnp.int32, (1, k), 1) == j
                pivot = jnp.sum(jnp.where(at, pivot_row, 0.0), axis=1, keepdims=True)
                column = jnp.sum(
                    jnp.where(at, rg[b * k : (b + 1) * k, b * k : (b + 1) * k], 0.0),
                    axis=1,
                    keepdims=True,
                )
                below = lax.broadcasted_iota(jnp.int32, (k, 1), 0) > j
                times = jnp.where(below, column / pivot, 0.0)
                rg[b * k : (b + 1) * k, b * k : (b + 1) * k] = (
                    rg[b * k : (b + 1) * k, b * k : (b + 1) * k] - times * pivot_row
                )
                w_ref[...] = w_ref[...] - times * unit_row
                w_ref[pl.ds(j, 1), :] = unit_row * lax.rsqrt(pivot)
                return carry

            lax.fori_loop(0, k, eliminate, 0)

        ws = split(w_ref[...] * lax.rsqrt(scale))
        below = (b + 1) * k
        new = nt3(split(rg[below:, b * k : (b + 1) * k]), ws)
        mine = new[total - below :]
        out_ref[:, b * k : (b + 1) * k] = mine
        new_diag = new_diag - jnp.sum(mine * mine, axis=1, keepdims=True)
        nh, nl = split(new)
        for c in range(b + 1, blocks):
            at = c * k - below
            rg[c * k :, c * k : (c + 1) * k] -= nt3(
                (nh[at:], nl[at:]), (nh[at : at + k], nl[at : at + k])
            )
    newdiag_ref[...] = new_diag


def on_device(n, sizes, orders, embeddings, factor, diagonal, pivot_owner, pivot_local):
    rows, width = embeddings.shape
    rank = factor.shape[1]
    blocks, pivots = pivot_owner.shape
    total = blocks * pivots
    device = lax.axis_index("rows") * lax.axis_size("sub") + lax.axis_index("sub")
    cap = sum(sizes)
    vmem = pl.BlockSpec(memory_space=pltpu.VMEM)
    smem = pl.BlockSpec(memory_space=pltpu.SMEM)
    anywhere = pl.BlockSpec(memory_space=pl.ANY)
    parts = pl.pallas_call(
        functools.partial(select_kernel, sizes),
        name="select_pivots",
        out_shape=[jax.ShapeDtypeStruct((size, width + rank), F32) for size in sizes],
        in_specs=[smem, vmem, vmem, vmem, vmem],
        out_specs=[vmem] * len(sizes),
    )(device.reshape(1), pivot_owner, pivot_local, embeddings, factor)

    def flip(bit, x):
        return lax.ppermute(x, AXES, [(d, d ^ (1 << bit)) for d in range(n)])

    parts = list(parts)
    for stage in range(len(orders[0])):
        for p, order in enumerate(orders):
            parts[p] = jnp.concatenate([parts[p], flip(order[stage], parts[p])], axis=0)
    buffers = parts + [flip(0, part) for part in parts]

    owner = pivot_owner.reshape(-1)
    order_of = jnp.arange(total)
    same = (owner[:, None] == owner[None, :]) & (order_of[None, :] < order_of[:, None])
    slot = jnp.sum(same.astype(jnp.int32), axis=1)
    relative = owner ^ device
    half = n // 2
    idx = jnp.zeros_like(slot)
    start, base = 0, 0
    for size, order in zip(sizes, orders, strict=True):
        place = jnp.zeros_like(slot)
        for i, bit in enumerate(order):
            place += ((relative >> bit) & 1) << i
        at = base + place * size + (slot - start)
        here = (slot >= start) & (slot < start + size)
        core = (relative & 1) * (half * cap)
        idx = jnp.where(here, at + core, idx)
        start += size
        base += half * size
    overflow = jnp.max(slot) >= cap

    def columns(idx, buffers):
        k = pivots
        return pl.pallas_call(
            functools.partial(main_kernel, width, blocks),
            name="pivot_blocks",
            out_shape=[
                jax.ShapeDtypeStruct((rows, total), F32),
                jax.ShapeDtypeStruct((rows, 1), F32),
            ],
            in_specs=[smem, vmem, vmem, vmem] + [anywhere] * len(buffers),
            out_specs=[vmem, vmem],
            scratch_shapes=[
                pltpu.VMEM((n * cap, width + rank), F32),
                pltpu.VMEM((total, width + rank), F32),
                pltpu.VMEM((total + rows, width), BF16),
                pltpu.VMEM((total + rows, rank), BF16),
                pltpu.VMEM((total + rows, rank), BF16),
                pltpu.VMEM((total + rows, 1), F32),
                pltpu.VMEM((total + rows, total), F32),
                pltpu.VMEM((k, k), F32),
                pltpu.SemaphoreType.DMA((len(buffers),)),
            ],
            compiler_params=pltpu.CompilerParams(vmem_limit_bytes=VMEM_LIMIT),
        )(idx, embeddings, factor, diagonal.reshape(rows, 1), *buffers)

    fast = columns(idx, buffers)

    def slow(fast):
        positions = lax.broadcasted_iota(jnp.int32, (total, rows), 1)
        hits = (owner[:, None] == device) & (pivot_local.reshape(-1)[:, None] == positions)
        hits = hits.astype(F32)
        points = jnp.dot(hits.astype(BF16), embeddings, preferred_element_type=F32)
        picked = jnp.dot(hits, factor, precision=lax.Precision.HIGHEST)
        everything = jnp.concatenate([points, picked], axis=1)
        for bit in range(n.bit_length() - 1):
            everything = everything + flip(bit, everything)
        everything = jnp.pad(everything, ((0, max(0, n * cap - total)), (0, 0)))
        pieces, start = [], 0
        for buffer in buffers:
            pieces.append(everything[start : start + buffer.shape[0]])
            start += buffer.shape[0]
        return columns(jnp.arange(total, dtype=jnp.int32), pieces)

    new_columns, new_diagonal = lax.cond(overflow, slow, lambda fast: fast, fast)
    return new_columns, new_diagonal.reshape(rows)


def solution(mesh):
    n = mesh.shape["rows"] * mesh.shape["sub"]

    def program(embeddings, factor, diagonal, pivot_owner, pivot_local):
        sizes, orders = plan(n, pivot_owner.size)
        spec = P(AXES)
        return jax.shard_map(
            functools.partial(on_device, n, sizes, orders),
            mesh=mesh,
            in_specs=(P(AXES, None), P(AXES, None), spec, P(), P()),
            out_specs=(P(AXES, None), spec),
            check_vma=False,
        )(embeddings, factor, diagonal, pivot_owner, pivot_local)

    return program
```

```python
import functools

import jax
import jax.numpy as jnp
from jax import lax
from jax.experimental import pallas as pl
from jax.experimental.pallas import tpu as pltpu
from jax.sharding import PartitionSpec as P

gamma_scale = 1.0
ridge_base = 0.5
AXES = ("rows", "sub")
F32 = jnp.float32
BF16 = jnp.bfloat16
TOL2 = 0.03 * 0.03
MAX_NEWTON = 12


def nt(a, b):
    return lax.dot_general(a, b, (((1,), (1,)), ((), ())), preferred_element_type=F32)


def nn(a, b):
    return lax.dot_general(a, b, (((1,), (0,)), ((), ())), preferred_element_type=F32)


def split(a):
    high = a.astype(BF16)
    return high, (a - high.astype(F32)).astype(BF16)


def nt3(a, b):
    return nt(a[0], b[0]) + (nt(a[0], b[1]) + nt(a[1], b[0]))


def nn3(a, b):
    return nn(a[0], b[0]) + (nn(a[0], b[1]) + nn(a[1], b[0]))


def row_sums(a):
    ones = jnp.ones((8, a.shape[1]), BF16)
    high, low = split(a)
    return (nt(ones, high) + nt(ones, low))[:1]


def plan(n, pivots):
    mean = pivots / n
    base = 8 * max(1, round(mean / 8))
    spare = 8 * max(1, -int(-(2.5 * mean**0.5) // 8))
    piece = min(base, 16)
    sizes = [piece] * (base // piece) + [base % piece] * (base % piece > 0) + [spare]
    bits = list(range(n.bit_length() - 2, 0, -1))
    orders = [bits]
    if len(bits) > 3:
        z2, z1, y, x = bits[:-3], bits[-3], bits[-2], bits[-1]
        orders = [z2 + [z1, y, x], z2 + [x, z1, y], z2 + [y, x, z1]]
    orders = [orders[p % len(orders)] for p in range(len(sizes))]
    return base, spare, sizes, orders


def select_kernel(sizes, me_ref, owner_ref, local_ref, emb_ref, fac_ref, *out_refs):
    me = me_ref[0]
    blocks, pivots = owner_ref.shape
    rows, width = emb_ref.shape
    spare = sizes[-1]
    base = sum(sizes) - spare
    total = base + 2 * spare
    padded = -(-total // 16) * 16
    before = lax.broadcasted_iota(jnp.int32, (pivots, pivots), 0) < lax.broadcasted_iota(
        jnp.int32, (pivots, pivots), 1
    )
    before = jnp.where(before, 1.0, 0.0).astype(BF16)
    mine = jnp.where(owner_ref[...] == me, 1.0, 0.0)
    partner = jnp.where(owner_ref[...] == (me ^ 1), 1.0, 0.0)
    prefix = nn(mine.astype(BF16), before)
    totals = jnp.sum(mine, axis=1, keepdims=True)
    slots = lax.broadcasted_iota(jnp.int32, (padded, 1), 0).astype(F32)
    odd = (me & 1).astype(F32)
    ahead = odd * jnp.maximum(jnp.sum(jnp.sum(partner, axis=1, keepdims=True), axis=0, keepdims=True) - base, 0.0)
    keeps = slots - ahead + odd * spare
    gives = slots - spare - ahead + (1.0 - odd) * spare
    rank = jnp.where(slots < base, slots, jnp.where(slots < base + spare, keeps, gives))
    rank = jnp.where((slots >= base) & (rank < base), -1.0, rank)
    where = jnp.full((padded, 1), -1.0, F32)
    offset = jnp.zeros((1, 1), F32)
    for b in range(blocks):
        slot = prefix[b : b + 1] + offset
        hit = (slot == rank) & (mine[b : b + 1] > 0.0)
        where += jnp.sum(
            jnp.where(hit, local_ref[b : b + 1, :].astype(F32) + 1.0, 0.0), axis=1, keepdims=True
        )
        offset = offset + totals[b : b + 1]
    positions = lax.broadcasted_iota(jnp.int32, (padded, rows), 1).astype(F32)
    onehot = jnp.where(where == positions, 1.0, 0.0).astype(BF16)
    points = nn(onehot, emb_ref[...])
    factor = fac_ref[...]
    high = factor.astype(BF16)
    rest = factor - high.astype(F32)
    middle, low = split(rest)
    picked = nn(onehot, high) + nn(onehot, middle) + nn(onehot, low)
    start = 0
    for out_ref in out_refs:
        size = out_ref.shape[0]
        out_ref[:, :width] = points[start : start + size]
        out_ref[:, width:] = picked[start : start + size]
        start += size


def main_kernel(
    width,
    blocks,
    idx_ref,
    emb_ref,
    fac_ref,
    diag_ref,
    *refs,
):
    nbuf = len(refs) - 2 - 9
    buf_refs = refs[:nbuf]
    out_ref, newdiag_ref = refs[nbuf : nbuf + 2]
    stage, gathered, e_ref, fh_ref, fl_ref, sq_ref, rg, w_ref, sem = refs[nbuf + 2 :]
    local = emb_ref.shape[0]
    total = idx_ref.shape[0]
    k = total // blocks
    copies = []
    start = 0
    for i, buf in enumerate(buf_refs):
        copies.append(
            pltpu.make_async_copy(buf, stage.at[pl.ds(start, buf.shape[0]), :], sem.at[i])
        )
        start += buf.shape[0]
    for copy in copies:
        copy.start()
    e_ref[total:, :] = emb_ref[...]
    high, low = split(fac_ref[...])
    fh_ref[total:, :] = high
    fl_ref[total:, :] = low
    wide = emb_ref[...].astype(F32)
    sq_ref[total:, :] = jnp.sum(wide * wide, axis=1, keepdims=True)
    for copy in copies:
        copy.wait()

    def gather(g, carry):
        for j in range(8):
            gathered[pl.ds(g * 8 + j, 1), :] = stage[pl.ds(idx_ref[g * 8 + j], 1), :]
        return carry

    lax.fori_loop(0, total // 8, gather, 0)
    row_squares = []
    for b in range(blocks):
        rows = pl.ds(b * k, k)
        wide = gathered[rows, :width]
        e_ref[rows, :] = wide.astype(BF16)
        high, low = split(gathered[rows, width:])
        fh_ref[rows, :] = high
        fl_ref[rows, :] = low
        square = wide * wide
        sq_ref[rows, :] = jnp.sum(square, axis=1, keepdims=True)
        row_squares.append(row_sums(square))
    for b in range(blocks):
        cols = pl.ds(b * k, k)
        eb, fb = e_ref[cols, :], (fh_ref[cols, :], fl_ref[cols, :])
        row_square = row_squares[b]

        def tile(t, carry, b=b, eb=eb, fb=fb, row_square=row_square):
            rows = pl.ds(pl.multiple_of(t * k, k), k)
            inner = nt(e_ref[rows, :], eb)
            kernel = jnp.exp(-gamma_scale * (sq_ref[rows, :] + row_square - 2.0 * inner))
            rg[rows, b * k : (b + 1) * k] = kernel - nt3((fh_ref[rows, :], fl_ref[rows, :]), fb)
            return carry

        lax.fori_loop(b, (total + local) // k, tile, 0)

    row = lax.broadcasted_iota(jnp.int32, (k, k), 0)
    col = lax.broadcasted_iota(jnp.int32, (k, k), 1)
    identity = jnp.where(row == col, 1.0, 0.0)
    lower = jnp.where(row > col, 1.0, 0.0) + 0.5 * identity
    new_diag = diag_ref[...]
    for b in range(blocks):
        gram = rg[b * k : (b + 1) * k, b * k : (b + 1) * k]
        diag = jnp.sum(gram * identity, axis=0, keepdims=True)
        off = jnp.sum(jnp.abs(gram), axis=0, keepdims=True) - jnp.abs(diag)
        shift = ridge_base + jnp.maximum(jnp.max(off - diag, axis=1, keepdims=True), 0.0)
        scale = shift + jnp.max(diag, axis=1, keepdims=True)
        shifted = (gram + shift * identity) / scale
        sh, sl = split(shifted)

        def update(error):
            f = error * lower
            fb = f.astype(BF16)
            return f - nn(fb, fb) - nt(fb, fb) * lower

        w = identity - update(shifted - identity)
        wb = w.astype(BF16)
        step = update(nt(nn(wb, sh).astype(BF16), wb) - identity)
        w = w - nn(step.astype(BF16), wb)

        def newton(w):
            ws = split(w)
            error = nt3(split(nn3(ws, (sh, sl))), ws) - identity
            w = w - nn3(split(update(error)), ws)
            return w, jnp.sum(error * error)

        w, norm = newton(w)
        w_ref[...] = w

        def more(state):
            i, norm = state
            return jnp.logical_and(i < MAX_NEWTON, jnp.logical_not(norm < TOL2))

        def again(state):
            i, norm = state
            w, norm = newton(w_ref[...])
            w_ref[...] = w
            return i + 1, norm

        _, norm = lax.while_loop(more, again, (0, norm))

        @pl.when(jnp.logical_not(norm < TOL2))
        def _():
            rg[b * k : (b + 1) * k, b * k : (b + 1) * k] = shifted
            w_ref[...] = identity

            def eliminate(j, carry):
                pivot_row = rg[pl.ds(b * k + j, 1), b * k : (b + 1) * k]
                unit_row = w_ref[pl.ds(j, 1), :]
                at = lax.broadcasted_iota(jnp.int32, (1, k), 1) == j
                pivot = jnp.sum(jnp.where(at, pivot_row, 0.0), axis=1, keepdims=True)
                column = jnp.sum(
                    jnp.where(at, rg[b * k : (b + 1) * k, b * k : (b + 1) * k], 0.0),
                    axis=1,
                    keepdims=True,
                )
                below = lax.broadcasted_iota(jnp.int32, (k, 1), 0) > j
                times = jnp.where(below, column / pivot, 0.0)
                rg[b * k : (b + 1) * k, b * k : (b + 1) * k] = (
                    rg[b * k : (b + 1) * k, b * k : (b + 1) * k] - times * pivot_row
                )
                w_ref[...] = w_ref[...] - times * unit_row
                w_ref[pl.ds(j, 1), :] = unit_row * lax.rsqrt(pivot)
                return carry

            lax.fori_loop(0, k, eliminate, 0)

        ws = split(w_ref[...] * lax.rsqrt(scale))
        below = (b + 1) * k
        new = nt3(split(rg[below:, b * k : (b + 1) * k]), ws)
        mine = new[total - below :]
        out_ref[:, b * k : (b + 1) * k] = mine
        new_diag = new_diag - row_sums(mine * mine)
        nh, nl = split(new)
        for c in range(b + 1, blocks):
            at = c * k - below
            rg[c * k :, c * k : (c + 1) * k] -= nt3(
                (nh[at:], nl[at:]), (nh[at : at + k], nl[at : at + k])
            )
    newdiag_ref[...] = new_diag


def on_device(n, base, spare, sizes, orders, embeddings, factor, diagonal, pivot_owner, pivot_local):
    rows, width = embeddings.shape
    rank = factor.shape[1]
    blocks, pivots = pivot_owner.shape
    total = blocks * pivots
    device = lax.axis_index("rows") * lax.axis_size("sub") + lax.axis_index("sub")
    cap = sum(sizes)
    vmem = pl.BlockSpec(memory_space=pltpu.VMEM)
    smem = pl.BlockSpec(memory_space=pltpu.SMEM)
    anywhere = pl.BlockSpec(memory_space=pl.ANY)
    *parts, give = pl.pallas_call(
        functools.partial(select_kernel, sizes),
        name="select_pivots",
        out_shape=[jax.ShapeDtypeStruct((size, width + rank), F32) for size in sizes + [spare]],
        in_specs=[smem, vmem, vmem, vmem, vmem],
        out_specs=[vmem] * (len(sizes) + 1),
    )(device.reshape(1), pivot_owner, pivot_local, embeddings, factor)

    def flip(bit, x):
        return lax.ppermute(x, AXES, [(d, d ^ (1 << bit)) for d in range(n)])

    parts[-1] = parts[-1] + flip(0, give)
    for stage in range(len(orders[0])):
        for p, order in enumerate(orders):
            parts[p] = jnp.concatenate([parts[p], flip(order[stage], parts[p])], axis=0)
    buffers = parts + [flip(0, part) for part in parts]

    owner = pivot_owner.reshape(-1)
    order_of = jnp.arange(total)
    same = owner[:, None] == owner[None, :]
    slot = jnp.sum((same & (order_of[None, :] < order_of[:, None])).astype(jnp.int32), axis=1)
    others = jnp.sum((owner[:, None] == (owner[None, :] ^ 1)).astype(jnp.int32), axis=1)
    shared = slot - base + (owner & 1) * jnp.maximum(others - base, 0)
    spilled = slot >= base
    overflow = jnp.max(jnp.where(spilled, shared, 0)) >= 2 * spare
    holder = jnp.where(spilled, (owner & ~1) | jnp.clip(shared // spare, 0, 1), owner)
    slot = jnp.where(spilled, base + shared % spare, slot)
    relative = holder ^ device
    half = n // 2
    idx = jnp.zeros_like(slot)
    start, begin = 0, 0
    for size, order in zip(sizes, orders, strict=True):
        place = jnp.zeros_like(slot)
        for i, bit in enumerate(order):
            place += ((relative >> bit) & 1) << i
        at = begin + place * size + (slot - start)
        here = (slot >= start) & (slot < start + size)
        idx = jnp.where(here, at + (relative & 1) * (half * cap), idx)
        start += size
        begin += half * size

    def columns(idx, buffers):
        k = pivots
        return pl.pallas_call(
            functools.partial(main_kernel, width, blocks),
            name="pivot_blocks",
            out_shape=[
                jax.ShapeDtypeStruct((rows, total), F32),
                jax.ShapeDtypeStruct((1, rows), F32),
            ],
            in_specs=[smem, vmem, vmem, vmem] + [anywhere] * len(buffers),
            out_specs=[vmem, vmem],
            scratch_shapes=[
                pltpu.VMEM((n * cap, width + rank), F32),
                pltpu.VMEM((total, width + rank), F32),
                pltpu.VMEM((total + rows, width), BF16),
                pltpu.VMEM((total + rows, rank), BF16),
                pltpu.VMEM((total + rows, rank), BF16),
                pltpu.VMEM((total + rows, 1), F32),
                pltpu.VMEM((total + rows, total), F32),
                pltpu.VMEM((k, k), F32),
                pltpu.SemaphoreType.DMA((len(buffers),)),
            ],
            compiler_params=pltpu.CompilerParams(vmem_limit_bytes=n * cap * (width + rank) * 4 + 24 * 1024 * 1024),
        )(idx, embeddings, factor, diagonal.reshape(1, rows), *buffers)

    def slow(idx, *buffers):
        positions = lax.broadcasted_iota(jnp.int32, (total, rows), 1)
        hits = (owner[:, None] == device) & (pivot_local.reshape(-1)[:, None] == positions)
        hits = hits.astype(F32)
        points = jnp.dot(hits.astype(BF16), embeddings, preferred_element_type=F32)
        picked = jnp.dot(hits, factor, precision=lax.Precision.HIGHEST)
        everything = jnp.concatenate([points, picked], axis=1)
        for bit in range(n.bit_length() - 1):
            everything = everything + flip(bit, everything)
        everything = jnp.pad(everything, ((0, max(0, n * cap - total)), (0, 0)))
        pieces, start = [], 0
        for buffer in buffers:
            pieces.append(everything[start : start + buffer.shape[0]])
            start += buffer.shape[0]
        return jnp.arange(total, dtype=jnp.int32), *pieces

    idx, *buffers = lax.cond(overflow, slow, lambda *held: held, idx, *buffers)
    new_columns, new_diagonal = columns(idx, buffers)
    return new_columns, new_diagonal.reshape(rows)


def solution(mesh):
    n = mesh.shape["rows"] * mesh.shape["sub"]

    def program(embeddings, factor, diagonal, pivot_owner, pivot_local):
        base, spare, sizes, orders = plan(n, pivot_owner.size)
        spec = P(AXES)
        return jax.shard_map(
            functools.partial(on_device, n, base, spare, sizes, orders),
            mesh=mesh,
            in_specs=(P(AXES, None), P(AXES, None), spec, P(), P()),
            out_specs=(P(AXES, None), spec),
            check_vma=False,
        )(embeddings, factor, diagonal, pivot_owner, pivot_local)

    return program
```

```python
import functools

import jax
import jax.numpy as jnp
from jax import lax
from jax.experimental import pallas as pl
from jax.experimental.pallas import tpu as pltpu
from jax.sharding import PartitionSpec as P

gamma_scale = 1.0
ridge_base = 0.5
AXES = ("rows", "sub")
F32 = jnp.float32
BF16 = jnp.bfloat16
TOL4 = 0.07**4
SPREAD = 1.35
MAX_NEWTON = 12


def nt(a, b):
    return lax.dot_general(a, b, (((1,), (1,)), ((), ())), preferred_element_type=F32)


def nn(a, b):
    return lax.dot_general(a, b, (((1,), (0,)), ((), ())), preferred_element_type=F32)


def split(a):
    high = a.astype(BF16)
    return high, (a - high.astype(F32)).astype(BF16)


def nt3(a, b):
    rows = a[0].shape[0]
    both = nt(jnp.concatenate(a, axis=0), b[0])
    return both[:rows] + (both[rows:] + nt(a[0], b[1]))


def nn3(a, b):
    rows = a[0].shape[0]
    both = nn(jnp.concatenate(a, axis=0), b[0])
    return both[:rows] + (both[rows:] + nn(a[0], b[1]))


def row_sums(a):
    ones = jnp.ones((8, a.shape[1]), BF16)
    high, low = split(a)
    return (nt(ones, high) + nt(ones, low))[:1]


def plan(n, pivots):
    mean = pivots / n
    base = 8 * max(1, round(mean / 8))
    spare = 8 * max(1, -int(-(2.5 * mean**0.5) // 8))
    piece = min(base, 16)
    sizes = [piece] * (base // piece) + [base % piece] * (base % piece > 0) + [spare]
    bits = list(range(n.bit_length() - 2, 0, -1))
    orders = [bits]
    if len(bits) > 3:
        z2, z1, y, x = bits[:-3], bits[-3], bits[-2], bits[-1]
        orders = [z2 + [z1, y, x], z2 + [x, z1, y], z2 + [y, x, z1]]
    orders = [orders[p % len(orders)] for p in range(len(sizes))]
    return base, spare, sizes, orders


def select_kernel(sizes, me_ref, owner_ref, local_ref, emb_ref, fac_ref, *out_refs):
    me = me_ref[0]
    blocks, pivots = owner_ref.shape
    rows, width = emb_ref.shape
    spare = sizes[-1]
    base = sum(sizes) - spare
    total = base + 2 * spare
    padded = -(-total // 16) * 16
    before = lax.broadcasted_iota(jnp.int32, (pivots, pivots), 0) < lax.broadcasted_iota(
        jnp.int32, (pivots, pivots), 1
    )
    before = jnp.where(before, 1.0, 0.0).astype(BF16)
    mine = jnp.where(owner_ref[...] == me, 1.0, 0.0)
    partner = jnp.where(owner_ref[...] == (me ^ 1), 1.0, 0.0)
    prefix = nn(mine.astype(BF16), before)
    totals = jnp.sum(mine, axis=1, keepdims=True)
    slots = lax.broadcasted_iota(jnp.int32, (padded, 1), 0).astype(F32)
    odd = (me & 1).astype(F32)
    ahead = odd * jnp.maximum(jnp.sum(jnp.sum(partner, axis=1, keepdims=True), axis=0, keepdims=True) - base, 0.0)
    keeps = slots - ahead + odd * spare
    gives = slots - spare - ahead + (1.0 - odd) * spare
    rank = jnp.where(slots < base, slots, jnp.where(slots < base + spare, keeps, gives))
    rank = jnp.where((slots >= base) & (rank < base), -1.0, rank)
    where = jnp.full((padded, 1), -1.0, F32)
    offset = jnp.zeros((1, 1), F32)
    for b in range(blocks):
        slot = prefix[b : b + 1] + offset
        hit = (slot == rank) & (mine[b : b + 1] > 0.0)
        where += jnp.sum(
            jnp.where(hit, local_ref[b : b + 1, :].astype(F32) + 1.0, 0.0), axis=1, keepdims=True
        )
        offset = offset + totals[b : b + 1]
    positions = lax.broadcasted_iota(jnp.int32, (padded, rows), 1).astype(F32)
    onehot = jnp.where(where == positions, 1.0, 0.0).astype(BF16)
    points = nn(onehot, emb_ref[...])
    factor = fac_ref[...]
    high = factor.astype(BF16)
    rest = factor - high.astype(F32)
    middle, low = split(rest)
    picked = nn(onehot, high) + nn(onehot, middle) + nn(onehot, low)
    start = 0
    for out_ref in out_refs:
        size = out_ref.shape[0]
        out_ref[:, :width] = points[start : start + size]
        out_ref[:, width:] = picked[start : start + size]
        start += size


def main_kernel(
    width,
    blocks,
    idx_ref,
    emb_ref,
    fac_ref,
    diag_ref,
    *refs,
):
    nbuf = len(refs) - 2 - 12
    buf_refs = refs[:nbuf]
    out_ref, newdiag_ref = refs[nbuf : nbuf + 2]
    stage, gathered, e_ref, fh_ref, fl_ref, sq_ref, rg, w_ref, wh_ref, wl_ref, sums, sem = refs[nbuf + 2 :]
    local = emb_ref.shape[0]
    total = idx_ref.shape[0]
    k = total // blocks
    rank = fac_ref.shape[1]
    copies = []
    start = 0
    for i, buf in enumerate(buf_refs):
        copies.append(
            pltpu.make_async_copy(buf, stage.at[pl.ds(start, buf.shape[0]), :], sem.at[i])
        )
        start += buf.shape[0]
    for copy in copies:
        copy.start()
    e_ref[total:, :] = emb_ref[...]
    high, low = split(fac_ref[...])
    fh_ref[total:, :rank] = high
    fl_ref[total:, :rank] = low
    wide = emb_ref[...].astype(F32)
    sq_ref[total:, :] = jnp.sum(wide * wide, axis=1, keepdims=True)
    for copy in copies:
        copy.wait()

    def gather(g, carry):
        for j in range(8):
            gathered[pl.ds(g * 8 + j, 1), :] = stage[pl.ds(idx_ref[g * 8 + j], 1), :]
        return carry

    lax.fori_loop(0, total // 8, gather, 0)
    row_squares = []
    for b in range(blocks):
        rows = pl.ds(b * k, k)
        wide = gathered[rows, :width]
        e_ref[rows, :] = wide.astype(BF16)
        high, low = split(gathered[rows, width:])
        fh_ref[rows, :rank] = high
        fl_ref[rows, :rank] = low
        square = wide * wide
        sq_ref[rows, :] = jnp.sum(square, axis=1, keepdims=True)
        row_squares.append(row_sums(square))
    tiles = (total + local) // k

    def tile(t, stop, b, known):
        cols = pl.ds(b * k, k)
        rows = pl.ds(t * k, (stop - t) * k)
        depth = rank + known * k
        inner = nt(e_ref[rows, :], e_ref[cols, :])
        kernel = jnp.exp(-gamma_scale * (sq_ref[rows, :] + row_squares[b] - 2.0 * inner))
        left = fh_ref[rows, :depth], fl_ref[rows, :depth]
        right = fh_ref[cols, :depth], fl_ref[cols, :depth]
        rg[rows, b * k : (b + 1) * k] = kernel - nt3(left, right)

    def columns(t, stop, b):
        rows = pl.ds(t * k, (stop - t) * k)
        new = nt3(split(rg[rows, b * k : (b + 1) * k]), (wh_ref[b], wl_ref[b]))
        if stop == tiles:
            mine = new[new.shape[0] - local :]
            out_ref[:, b * k : (b + 1) * k] = mine
            sums[b] = row_sums(mine * mine)
        if b + 1 < blocks:
            high, low = split(new)
            fh_ref[rows, rank + b * k : rank + (b + 1) * k] = high
            fl_ref[rows, rank + b * k : rank + (b + 1) * k] = low
            return high, low

    row = lax.broadcasted_iota(jnp.int32, (k, k), 0)
    col = lax.broadcasted_iota(jnp.int32, (k, k), 1)
    identity = jnp.where(row == col, 1.0, 0.0)
    lower = jnp.where(row > col, 1.0, 0.0) + 0.5 * identity
    tile(0, 1, 0, 0)
    for b in range(blocks):
        ahead = []
        if b > 0:
            ahead.append(functools.partial(columns, b + 1, tiles, b - 1))
        if b + 1 < blocks:
            ahead.append(functools.partial(tile, b + 1, b + 2, b + 1, b))
        middle = (b + 1 + tiles) // 2
        ahead.append(functools.partial(tile, b + 1, middle, b, b))
        ahead.append(functools.partial(tile, middle, tiles, b, b))
        quarter = -(-len(ahead) // 4)

        def filler(ahead=ahead, quarter=quarter):
            for _ in range(min(quarter, len(ahead))):
                ahead.pop(0)()

        gram = rg[b * k : (b + 1) * k, b * k : (b + 1) * k]
        diag = jnp.sum(gram * identity, axis=0, keepdims=True)
        off = jnp.sum(jnp.abs(gram), axis=0, keepdims=True) - jnp.abs(diag)
        shift = ridge_base + jnp.maximum(jnp.max(off - diag, axis=1, keepdims=True), 0.0)
        scale = SPREAD * (shift + jnp.max(diag, axis=1, keepdims=True))
        shifted = (gram + shift * identity) / scale
        sh, sl = split(shifted)

        def update(error):
            f = error * lower
            fb = f.astype(BF16)
            return f - nn(fb, fb) - nt(fb, fb) * lower

        def newton(away, fill):
            ws = split(identity - away)
            product = split(nn3(ws, (sh, sl)))
            fill()
            error = nt3(product, ws) - identity
            fill()
            step = update(error)
            fill()
            moved = step - nn(step.astype(BF16), away.astype(BF16))
            eb = error.astype(BF16)
            twice = nt(eb, eb)
            return away + moved, jnp.sum(twice * twice)

        away = update(shifted - identity)
        filler()
        away, norm = newton(away, filler)
        while ahead:
            filler()
        w_ref[...] = away

        def more(state):
            i, norm = state
            return jnp.logical_and(i < MAX_NEWTON, jnp.logical_not(norm < TOL4))

        def again(state):
            i, norm = state
            away, norm = newton(w_ref[...], lambda: None)
            w_ref[...] = away
            return i + 1, norm

        _, norm = lax.while_loop(more, again, (0, norm))
        w_ref[...] = identity - w_ref[...]

        @pl.when(jnp.logical_not(norm < TOL4))
        def _():
            left = rg.at[b * k : (b + 1) * k, b * k : (b + 1) * k]
            left[...] = shifted
            w_ref[...] = identity

            def eliminate(j, carry):
                pivot_row = left[pl.ds(j, 1), :]
                unit_row = w_ref[pl.ds(j, 1), :]
                at = lax.broadcasted_iota(jnp.int32, (1, k), 1) == j
                pivot = jnp.sum(jnp.where(at, pivot_row, 0.0), axis=1, keepdims=True)
                column = jnp.sum(jnp.where(at, left[...], 0.0), axis=1, keepdims=True)
                below = lax.broadcasted_iota(jnp.int32, (k, 1), 0) > j
                times = jnp.where(below, column / pivot, 0.0)
                left[...] = left[...] - times * pivot_row
                w_ref[...] = w_ref[...] - times * unit_row
                w_ref[pl.ds(j, 1), :] = unit_row * lax.rsqrt(pivot)
                return carry

            lax.fori_loop(0, k, eliminate, 0)

        wh_ref[b], wl_ref[b] = split(w_ref[...] * lax.rsqrt(scale))
        if b + 1 < blocks:
            new = columns(b + 1, b + 2, b)
            at = slice((b + 1) * k, (b + 2) * k)
            rg[at, at] -= nt3(new, new)
        else:
            columns(b + 1, tiles, b)
    newdiag_ref[...] = diag_ref[...] - functools.reduce(jnp.add, [sums[b] for b in range(blocks)])


def on_device(n, base, spare, sizes, orders, embeddings, factor, diagonal, pivot_owner, pivot_local):
    rows, width = embeddings.shape
    rank = factor.shape[1]
    blocks, pivots = pivot_owner.shape
    total = blocks * pivots
    device = lax.axis_index("rows") * lax.axis_size("sub") + lax.axis_index("sub")
    cap = sum(sizes)
    vmem = pl.BlockSpec(memory_space=pltpu.VMEM)
    smem = pl.BlockSpec(memory_space=pltpu.SMEM)
    anywhere = pl.BlockSpec(memory_space=pl.ANY)
    *parts, give = pl.pallas_call(
        functools.partial(select_kernel, sizes),
        name="select_pivots",
        out_shape=[jax.ShapeDtypeStruct((size, width + rank), F32) for size in sizes + [spare]],
        in_specs=[smem, vmem, vmem, vmem, vmem],
        out_specs=[vmem] * (len(sizes) + 1),
    )(device.reshape(1), pivot_owner, pivot_local, embeddings, factor)

    def flip(bit, x):
        return lax.ppermute(x, AXES, [(d, d ^ (1 << bit)) for d in range(n)])

    parts[-1] = parts[-1] + flip(0, give)
    last = len(orders[0]) - 1
    for stage in range(last):
        for p, order in enumerate(orders):
            parts[p] = jnp.concatenate([parts[p], flip(order[stage], parts[p])], axis=0)
    buffers = []
    for part, order in zip(parts, orders, strict=True):
        buffers += [part, flip(order[last], part)]
    buffers += [flip(0, buffer) for buffer in buffers]

    owner = pivot_owner.reshape(-1)
    order_of = jnp.arange(total)
    same = owner[:, None] == owner[None, :]
    slot = jnp.sum((same & (order_of[None, :] < order_of[:, None])).astype(jnp.int32), axis=1)
    others = jnp.sum((owner[:, None] == (owner[None, :] ^ 1)).astype(jnp.int32), axis=1)
    shared = slot - base + (owner & 1) * jnp.maximum(others - base, 0)
    spilled = slot >= base
    overflow = jnp.max(jnp.where(spilled, shared, 0)) >= 2 * spare
    holder = jnp.where(spilled, (owner & ~1) | jnp.clip(shared // spare, 0, 1), owner)
    slot = jnp.where(spilled, base + shared % spare, slot)
    relative = holder ^ device
    half = n // 2
    idx = jnp.zeros_like(slot)
    start, begin = 0, 0
    for size, order in zip(sizes, orders, strict=True):
        place = jnp.zeros_like(slot)
        for i, bit in enumerate(order):
            place += ((relative >> bit) & 1) << i
        at = begin + place * size + (slot - start)
        here = (slot >= start) & (slot < start + size)
        idx = jnp.where(here, at + (relative & 1) * (half * cap), idx)
        start += size
        begin += half * size

    def run_blocks(idx, buffers):
        k = pivots
        return pl.pallas_call(
            functools.partial(main_kernel, width, blocks),
            name="pivot_blocks",
            out_shape=[
                jax.ShapeDtypeStruct((rows, total), F32),
                jax.ShapeDtypeStruct((1, rows), F32),
            ],
            in_specs=[smem, vmem, vmem, vmem] + [anywhere] * len(buffers),
            out_specs=[vmem, vmem],
            scratch_shapes=[
                pltpu.VMEM((n * cap, width + rank), F32),
                pltpu.VMEM((total, width + rank), F32),
                pltpu.VMEM((total + rows, width), BF16),
                pltpu.VMEM((total + rows, rank + total - k), BF16),
                pltpu.VMEM((total + rows, rank + total - k), BF16),
                pltpu.VMEM((total + rows, 1), F32),
                pltpu.VMEM((total + rows, total), F32),
                pltpu.VMEM((k, k), F32),
                pltpu.VMEM((blocks, k, k), BF16),
                pltpu.VMEM((blocks, k, k), BF16),
                pltpu.VMEM((blocks, 1, rows), F32),
                pltpu.SemaphoreType.DMA((len(buffers),)),
            ],
            compiler_params=pltpu.CompilerParams(vmem_limit_bytes=n * cap * (width + rank) * 4 + 36 * 1024 * 1024),
        )(idx, embeddings, factor, diagonal.reshape(1, rows), *buffers)

    def slow(idx, *buffers):
        positions = lax.broadcasted_iota(jnp.int32, (total, rows), 1)
        hits = (owner[:, None] == device) & (pivot_local.reshape(-1)[:, None] == positions)
        hits = hits.astype(F32)
        points = jnp.dot(hits.astype(BF16), embeddings, preferred_element_type=F32)
        picked = jnp.dot(hits, factor, precision=lax.Precision.HIGHEST)
        everything = jnp.concatenate([points, picked], axis=1)
        for bit in range(n.bit_length() - 1):
            everything = everything + flip(bit, everything)
        everything = jnp.pad(everything, ((0, max(0, n * cap - total)), (0, 0)))
        pieces, start = [], 0
        for buffer in buffers:
            pieces.append(everything[start : start + buffer.shape[0]])
            start += buffer.shape[0]
        return jnp.arange(total, dtype=jnp.int32), *pieces

    idx, *buffers = lax.cond(overflow, slow, lambda *held: held, idx, *buffers)
    new_columns, new_diagonal = run_blocks(idx, buffers)
    return new_columns, new_diagonal.reshape(rows)


def solution(mesh):
    n = mesh.shape["rows"] * mesh.shape["sub"]

    def program(embeddings, factor, diagonal, pivot_owner, pivot_local):
        base, spare, sizes, orders = plan(n, pivot_owner.size)
        spec = P(AXES)
        return jax.shard_map(
            functools.partial(on_device, n, base, spare, sizes, orders),
            mesh=mesh,
            in_specs=(P(AXES, None), P(AXES, None), spec, P(), P()),
            out_specs=(P(AXES, None), spec),
            check_vma=False,
        )(embeddings, factor, diagonal, pivot_owner, pivot_local)

    return program
```

```python
import functools

import jax
import jax.numpy as jnp
from jax import lax
from jax.experimental import pallas as pl
from jax.experimental.pallas import tpu as pltpu
from jax.sharding import PartitionSpec as P

gamma_scale = 1.0
ridge_base = 0.5
AXES = ("rows", "sub")
F32 = jnp.float32
BF16 = jnp.bfloat16
TOL4 = 0.07**4
SPREAD = 1.35
MAX_NEWTON = 12


def nt(a, b):
    return lax.dot_general(a, b, (((1,), (1,)), ((), ())), preferred_element_type=F32)


def nn(a, b):
    return lax.dot_general(a, b, (((1,), (0,)), ((), ())), preferred_element_type=F32)


def split(a):
    high = a.astype(BF16)
    return high, (a - high.astype(F32)).astype(BF16)


def nt3(a, b):
    rows = a[0].shape[0]
    both = nt(jnp.concatenate(a, axis=0), b[0])
    return both[:rows] + (both[rows:] + nt(a[0], b[1]))


def nn3(a, b):
    rows = a[0].shape[0]
    both = nn(jnp.concatenate(a, axis=0), b[0])
    return both[:rows] + (both[rows:] + nn(a[0], b[1]))


def row_sums(a):
    ones = jnp.ones((8, a.shape[1]), BF16)
    high, low = split(a)
    return (nt(ones, high) + nt(ones, low))[:1]


def plan(n, pivots):
    mean = pivots / n
    base = 8 * max(1, round(mean / 8))
    spare = 8 * max(1, -int(-(2.5 * mean**0.5) // 8))
    piece = min(base, 16)
    sizes = [piece] * (base // piece) + [base % piece] * (base % piece > 0) + [spare]
    bits = list(range(n.bit_length() - 2, 0, -1))
    orders = [bits]
    if len(bits) > 3:
        z2, z1, y, x = bits[:-3], bits[-3], bits[-2], bits[-1]
        orders = [z2 + [z1, y, x], z2 + [x, z1, y], z2 + [y, x, z1]]
    orders = [orders[p % len(orders)] for p in range(len(sizes))]
    return base, spare, sizes, orders


def select_kernel(sizes, me_ref, owner_ref, local_ref, emb_ref, fac_ref, *out_refs):
    me = me_ref[0]
    blocks, pivots = owner_ref.shape
    rows, width = emb_ref.shape
    spare = sizes[-1]
    base = sum(sizes) - spare
    total = base + 2 * spare
    padded = -(-total // 16) * 16
    before = lax.broadcasted_iota(jnp.int32, (pivots, pivots), 0) < lax.broadcasted_iota(
        jnp.int32, (pivots, pivots), 1
    )
    before = jnp.where(before, 1.0, 0.0).astype(BF16)
    mine = jnp.where(owner_ref[...] == me, 1.0, 0.0)
    partner = jnp.where(owner_ref[...] == (me ^ 1), 1.0, 0.0)
    prefix = nn(mine.astype(BF16), before)
    totals = jnp.sum(mine, axis=1, keepdims=True)
    slots = lax.broadcasted_iota(jnp.int32, (padded, 1), 0).astype(F32)
    odd = (me & 1).astype(F32)
    ahead = odd * jnp.maximum(jnp.sum(jnp.sum(partner, axis=1, keepdims=True), axis=0, keepdims=True) - base, 0.0)
    keeps = slots - ahead + odd * spare
    gives = slots - spare - ahead + (1.0 - odd) * spare
    rank = jnp.where(slots < base, slots, jnp.where(slots < base + spare, keeps, gives))
    rank = jnp.where((slots >= base) & (rank < base), -1.0, rank)
    where = jnp.full((padded, 1), -1.0, F32)
    offset = jnp.zeros((1, 1), F32)
    for b in range(blocks):
        slot = prefix[b : b + 1] + offset
        hit = (slot == rank) & (mine[b : b + 1] > 0.0)
        where += jnp.sum(
            jnp.where(hit, local_ref[b : b + 1, :].astype(F32) + 1.0, 0.0), axis=1, keepdims=True
        )
        offset = offset + totals[b : b + 1]
    positions = lax.broadcasted_iota(jnp.int32, (padded, rows), 1).astype(F32)
    onehot = jnp.where(where == positions, 1.0, 0.0).astype(BF16)
    points = nn(onehot, emb_ref[...])
    high, low = split(fac_ref[...])
    picked = nn(onehot, high) + nn(onehot, low)
    start = 0
    for out_ref in out_refs:
        size = out_ref.shape[0]
        out_ref[:, :width] = points[start : start + size]
        out_ref[:, width:] = picked[start : start + size]
        start += size


def main_kernel(
    width,
    blocks,
    idx_ref,
    emb_ref,
    fac_ref,
    diag_ref,
    *refs,
):
    nbuf = len(refs) - 2 - 12
    buf_refs = refs[:nbuf]
    out_ref, newdiag_ref = refs[nbuf : nbuf + 2]
    stage, gathered, e_ref, fh_ref, fl_ref, sq_ref, rg, w_ref, wh_ref, wl_ref, sums, sem = refs[nbuf + 2 :]
    local = emb_ref.shape[0]
    total = idx_ref.shape[0]
    k = total // blocks
    rank = fac_ref.shape[1]
    copies = []
    start = 0
    for i, buf in enumerate(buf_refs):
        copies.append(
            pltpu.make_async_copy(buf, stage.at[pl.ds(start, buf.shape[0]), :], sem.at[i])
        )
        start += buf.shape[0]
    for copy in copies:
        copy.start()
    e_ref[total:, :] = emb_ref[...]
    high, low = split(fac_ref[...])
    fh_ref[total:, :rank] = high
    fl_ref[total:, :rank] = low
    wide = emb_ref[...].astype(F32)
    sq_ref[total:, :] = jnp.sum(wide * wide, axis=1, keepdims=True)
    for copy in copies:
        copy.wait()

    row_squares = [None] * blocks

    def gather(b, unrolled):
        def some(g, carry):
            for j in range(8):
                at = b * k + g * 8 + j
                gathered[pl.ds(at, 1), :] = stage[pl.ds(idx_ref[at], 1), :]
            return carry

        if unrolled:
            for g in range(k // 8):
                some(g, 0)
        else:
            lax.fori_loop(0, k // 8, some, 0)

    def prepare(b):
        rows = pl.ds(b * k, k)
        wide = gathered[rows, :width]
        e_ref[rows, :] = wide.astype(BF16)
        high, low = split(gathered[rows, width:])
        fh_ref[rows, :rank] = high
        fl_ref[rows, :rank] = low
        square = wide * wide
        sq_ref[rows, :] = jnp.sum(square, axis=1, keepdims=True)
        row_squares[b] = row_sums(square)

    unroll = True
    gather(0, False)
    if not unroll:
        for b in range(1, blocks):
            gather(b, False)
    prepare(0)
    tiles = (total + local) // k

    def tile(t, stop, b, known):
        cols = pl.ds(b * k, k)
        rows = pl.ds(t * k, (stop - t) * k)
        depth = rank + known * k
        inner = nt(e_ref[rows, :], e_ref[cols, :])
        kernel = jnp.exp(-gamma_scale * (sq_ref[rows, :] + row_squares[b] - 2.0 * inner))
        left = fh_ref[rows, :depth], fl_ref[rows, :depth]
        right = fh_ref[cols, :depth], fl_ref[cols, :depth]
        rg[rows, b * k : (b + 1) * k] = kernel - nt3(left, right)

    def columns(t, stop, b):
        rows = pl.ds(t * k, (stop - t) * k)
        new = nt3(split(rg[rows, b * k : (b + 1) * k]), (wh_ref[b], wl_ref[b]))
        if stop == tiles:
            mine = new[new.shape[0] - local :]
            out_ref[:, b * k : (b + 1) * k] = mine
            sums[b] = row_sums(mine * mine)
        if b + 1 < blocks:
            high, low = split(new)
            fh_ref[rows, rank + b * k : rank + (b + 1) * k] = high
            fl_ref[rows, rank + b * k : rank + (b + 1) * k] = low
            return high, low

    row = lax.broadcasted_iota(jnp.int32, (k, k), 0)
    col = lax.broadcasted_iota(jnp.int32, (k, k), 1)
    identity = jnp.where(row == col, 1.0, 0.0)
    lower = jnp.where(row > col, 1.0, 0.0) + 0.5 * identity
    tile(0, 1, 0, 0)
    for b in range(blocks):
        ahead = []
        if b == 0:
            ahead.append(functools.partial(tile, blocks, tiles, 0, 0))
            for c in range(1, blocks):
                if unroll:
                    ahead.append(functools.partial(gather, c, True))
                ahead.append(functools.partial(prepare, c))
            ahead.append(functools.partial(tile, 1, blocks, 0, 0))
            ahead.append(functools.partial(tile, 1, 2, 1, 0))
        else:
            ahead.append(functools.partial(columns, b + 1, tiles, b - 1))
            if b + 1 < blocks:
                ahead.append(functools.partial(tile, b + 1, b + 2, b + 1, b))
            middle = (b + 1 + tiles) // 2
            ahead.append(functools.partial(tile, b + 1, middle, b, b))
            ahead.append(functools.partial(tile, middle, tiles, b, b))
        quarter = -(-len(ahead) // 4)

        def filler(ahead=ahead, quarter=quarter):
            for _ in range(min(quarter, len(ahead))):
                ahead.pop(0)()

        gram = rg[b * k : (b + 1) * k, b * k : (b + 1) * k]
        diag = jnp.sum(gram * identity, axis=0, keepdims=True)
        off = jnp.sum(jnp.abs(gram), axis=0, keepdims=True) - jnp.abs(diag)
        shift = ridge_base + jnp.maximum(jnp.max(off - diag, axis=1, keepdims=True), 0.0)
        scale = SPREAD * (shift + jnp.max(diag, axis=1, keepdims=True))
        shifted = (gram + shift * identity) / scale
        sh, sl = split(shifted)

        def update(error):
            f = error * lower
            fb = f.astype(BF16)
            return f - nn(fb, fb) - nt(fb, fb) * lower

        def newton(away, fill):
            ws = split(identity - away)
            product = split(nn3(ws, (sh, sl)))
            fill()
            error = nt3(product, ws) - identity
            fill()
            step = update(error)
            fill()
            moved = step - nn(step.astype(BF16), away.astype(BF16))
            eb = error.astype(BF16)
            twice = nt(eb, eb)
            return away + moved, jnp.sum(twice * twice)

        away = update(shifted - identity)
        filler()
        away, norm = newton(away, filler)
        while ahead:
            filler()
        w_ref[...] = away

        def more(state):
            i, norm = state
            return jnp.logical_and(i < MAX_NEWTON, jnp.logical_not(norm < TOL4))

        def again(state):
            i, norm = state
            away, norm = newton(w_ref[...], lambda: None)
            w_ref[...] = away
            return i + 1, norm

        _, norm = lax.while_loop(more, again, (0, norm))
        w_ref[...] = identity - w_ref[...]

        @pl.when(jnp.logical_not(norm < TOL4))
        def _():
            left = rg.at[b * k : (b + 1) * k, b * k : (b + 1) * k]
            left[...] = shifted
            w_ref[...] = identity

            def eliminate(j, carry):
                pivot_row = left[pl.ds(j, 1), :]
                unit_row = w_ref[pl.ds(j, 1), :]
                at = lax.broadcasted_iota(jnp.int32, (1, k), 1) == j
                pivot = jnp.sum(jnp.where(at, pivot_row, 0.0), axis=1, keepdims=True)
                column = jnp.sum(jnp.where(at, left[...], 0.0), axis=1, keepdims=True)
                below = lax.broadcasted_iota(jnp.int32, (k, 1), 0) > j
                times = jnp.where(below, column / pivot, 0.0)
                left[...] = left[...] - times * pivot_row
                w_ref[...] = w_ref[...] - times * unit_row
                w_ref[pl.ds(j, 1), :] = unit_row * lax.rsqrt(pivot)
                return carry

            lax.fori_loop(0, k, eliminate, 0)

        wh_ref[b], wl_ref[b] = split(w_ref[...] * lax.rsqrt(scale))
        if b + 1 < blocks:
            new = columns(b + 1, b + 2, b)
            at = slice((b + 1) * k, (b + 2) * k)
            rg[at, at] -= nt3(new, new)
        else:
            columns(b + 1, tiles, b)
    newdiag_ref[...] = diag_ref[...] - functools.reduce(jnp.add, [sums[b] for b in range(blocks)])


def on_device(n, base, spare, sizes, orders, embeddings, factor, diagonal, pivot_owner, pivot_local):
    rows, width = embeddings.shape
    rank = factor.shape[1]
    blocks, pivots = pivot_owner.shape
    total = blocks * pivots
    device = lax.axis_index("rows") * lax.axis_size("sub") + lax.axis_index("sub")
    cap = sum(sizes)
    vmem = pl.BlockSpec(memory_space=pltpu.VMEM)
    smem = pl.BlockSpec(memory_space=pltpu.SMEM)
    anywhere = pl.BlockSpec(memory_space=pl.ANY)
    *parts, give = pl.pallas_call(
        functools.partial(select_kernel, sizes),
        name="select_pivots",
        out_shape=[jax.ShapeDtypeStruct((size, width + rank), F32) for size in sizes + [spare]],
        in_specs=[smem, vmem, vmem, vmem, vmem],
        out_specs=[vmem] * (len(sizes) + 1),
    )(device.reshape(1), pivot_owner, pivot_local, embeddings, factor)

    def flip(bit, x):
        return lax.ppermute(x, AXES, [(d, d ^ (1 << bit)) for d in range(n)])

    parts[-1] = parts[-1] + flip(0, give)
    last = len(orders[0]) - 1
    for stage in range(last):
        for p, order in enumerate(orders):
            parts[p] = jnp.concatenate([parts[p], flip(order[stage], parts[p])], axis=0)
    buffers = []
    for part, order in zip(parts, orders, strict=True):
        buffers += [part, flip(order[last], part)]
    buffers += [flip(0, buffer) for buffer in buffers]

    owner = pivot_owner.reshape(-1)
    order_of = jnp.arange(total)
    same = owner[:, None] == owner[None, :]
    slot = jnp.sum((same & (order_of[None, :] < order_of[:, None])).astype(jnp.int32), axis=1)
    others = jnp.sum((owner[:, None] == (owner[None, :] ^ 1)).astype(jnp.int32), axis=1)
    shared = slot - base + (owner & 1) * jnp.maximum(others - base, 0)
    spilled = slot >= base
    overflow = jnp.max(jnp.where(spilled, shared, 0)) >= 2 * spare
    holder = jnp.where(spilled, (owner & ~1) | jnp.clip(shared // spare, 0, 1), owner)
    slot = jnp.where(spilled, base + shared % spare, slot)
    relative = holder ^ device
    half = n // 2
    idx = jnp.zeros_like(slot)
    start, begin = 0, 0
    for size, order in zip(sizes, orders, strict=True):
        place = jnp.zeros_like(slot)
        for i, bit in enumerate(order):
            place += ((relative >> bit) & 1) << i
        at = begin + place * size + (slot - start)
        here = (slot >= start) & (slot < start + size)
        idx = jnp.where(here, at + (relative & 1) * (half * cap), idx)
        start += size
        begin += half * size

    def run_blocks(idx, buffers):
        k = pivots
        return pl.pallas_call(
            functools.partial(main_kernel, width, blocks),
            name="pivot_blocks",
            out_shape=[
                jax.ShapeDtypeStruct((rows, total), F32),
                jax.ShapeDtypeStruct((1, rows), F32),
            ],
            in_specs=[smem, vmem, vmem, vmem] + [anywhere] * len(buffers),
            out_specs=[vmem, vmem],
            scratch_shapes=[
                pltpu.VMEM((n * cap, width + rank), F32),
                pltpu.VMEM((total, width + rank), F32),
                pltpu.VMEM((total + rows, width), BF16),
                pltpu.VMEM((total + rows, rank + total - k), BF16),
                pltpu.VMEM((total + rows, rank + total - k), BF16),
                pltpu.VMEM((total + rows, 1), F32),
                pltpu.VMEM((total + rows, total), F32),
                pltpu.VMEM((k, k), F32),
                pltpu.VMEM((blocks, k, k), BF16),
                pltpu.VMEM((blocks, k, k), BF16),
                pltpu.VMEM((blocks, 1, rows), F32),
                pltpu.SemaphoreType.DMA((len(buffers),)),
            ],
            compiler_params=pltpu.CompilerParams(vmem_limit_bytes=n * cap * (width + rank) * 4 + 36 * 1024 * 1024),
        )(idx, embeddings, factor, diagonal.reshape(1, rows), *buffers)

    def slow(idx, *buffers):
        positions = lax.broadcasted_iota(jnp.int32, (total, rows), 1)
        hits = (owner[:, None] == device) & (pivot_local.reshape(-1)[:, None] == positions)
        hits = hits.astype(F32)
        points = jnp.dot(hits.astype(BF16), embeddings, preferred_element_type=F32)
        picked = jnp.dot(hits, factor, precision=lax.Precision.HIGHEST)
        everything = jnp.concatenate([points, picked], axis=1)
        for bit in range(n.bit_length() - 1):
            everything = everything + flip(bit, everything)
        everything = jnp.pad(everything, ((0, max(0, n * cap - total)), (0, 0)))
        pieces, start = [], 0
        for buffer in buffers:
            pieces.append(everything[start : start + buffer.shape[0]])
            start += buffer.shape[0]
        return jnp.arange(total, dtype=jnp.int32), *pieces

    idx, *buffers = lax.cond(overflow, slow, lambda *held: held, idx, *buffers)
    new_columns, new_diagonal = run_blocks(idx, buffers)
    return new_columns, new_diagonal.reshape(rows)


def solution(mesh):
    n = mesh.shape["rows"] * mesh.shape["sub"]

    def program(embeddings, factor, diagonal, pivot_owner, pivot_local):
        base, spare, sizes, orders = plan(n, pivot_owner.size)
        spec = P(AXES)
        return jax.shard_map(
            functools.partial(on_device, n, base, spare, sizes, orders),
            mesh=mesh,
            in_specs=(P(AXES, None), P(AXES, None), spec, P(), P()),
            out_specs=(P(AXES, None), spec),
            check_vma=False,
        )(embeddings, factor, diagonal, pivot_owner, pivot_local)

    return program
```

```python
import functools

import jax
import jax.numpy as jnp
from jax import lax
from jax.experimental import pallas as pl
from jax.experimental.pallas import tpu as pltpu
from jax.sharding import PartitionSpec as P

gamma_scale = 1.0
ridge_base = 0.5
AXES = ("rows", "sub")
F32 = jnp.float32
BF16 = jnp.bfloat16
TOL4 = 0.07**4
SPREAD = 1.35
MAX_NEWTON = 12


def nt(a, b):
    return lax.dot_general(a, b, (((1,), (1,)), ((), ())), preferred_element_type=F32)


def nn(a, b):
    return lax.dot_general(a, b, (((1,), (0,)), ((), ())), preferred_element_type=F32)


def split(a):
    high = a.astype(BF16)
    return high, (a - high.astype(F32)).astype(BF16)


def nt3(a, b):
    rows = a[0].shape[0]
    both = nt(jnp.concatenate(a, axis=0), b[0])
    return both[:rows] + (both[rows:] + nt(a[0], b[1]))


def nn3(a, b):
    rows = a[0].shape[0]
    both = nn(jnp.concatenate(a, axis=0), b[0])
    return both[:rows] + (both[rows:] + nn(a[0], b[1]))


def row_sums(a):
    ones = jnp.ones((8, a.shape[1]), BF16)
    high, low = split(a)
    return (nt(ones, high) + nt(ones, low))[:1]


def plan(n, pivots):
    mean = pivots / n
    base = 8 * max(1, round(mean / 8))
    spare = 8 * max(1, -int(-(2.5 * mean**0.5) // 8))
    piece = min(base, 16)
    sizes = [piece] * (base // piece) + [base % piece] * (base % piece > 0) + [spare]
    bits = list(range(n.bit_length() - 2, 0, -1))
    orders = [bits]
    if len(bits) > 3:
        z2, z1, y, x = bits[:-3], bits[-3], bits[-2], bits[-1]
        orders = [z2 + [z1, y, x], z2 + [x, z1, y], z2 + [y, x, z1]]
    orders = [orders[p % len(orders)] for p in range(len(sizes))]
    return base, spare, sizes, orders


def select_kernel(sizes, me_ref, owner_ref, local_ref, emb_ref, fac_ref, *out_refs):
    me = me_ref[0]
    blocks, pivots = owner_ref.shape
    rows, width = emb_ref.shape
    spare = sizes[-1]
    base = sum(sizes) - spare
    total = base + 2 * spare
    padded = -(-total // 16) * 16
    before = lax.broadcasted_iota(jnp.int32, (pivots, pivots), 0) < lax.broadcasted_iota(
        jnp.int32, (pivots, pivots), 1
    )
    before = jnp.where(before, 1.0, 0.0).astype(BF16)
    mine = jnp.where(owner_ref[...] == me, 1.0, 0.0)
    partner = jnp.where(owner_ref[...] == (me ^ 1), 1.0, 0.0)
    prefix = nn(mine.astype(BF16), before)
    totals = jnp.sum(mine, axis=1, keepdims=True)
    slots = lax.broadcasted_iota(jnp.int32, (padded, 1), 0).astype(F32)
    odd = (me & 1).astype(F32)
    ahead = odd * jnp.maximum(jnp.sum(jnp.sum(partner, axis=1, keepdims=True), axis=0, keepdims=True) - base, 0.0)
    keeps = slots - ahead + odd * spare
    gives = slots - spare - ahead + (1.0 - odd) * spare
    rank = jnp.where(slots < base, slots, jnp.where(slots < base + spare, keeps, gives))
    rank = jnp.where((slots >= base) & (rank < base), -1.0, rank)
    where = jnp.full((padded, 1), -1.0, F32)
    offset = jnp.zeros((1, 1), F32)
    for b in range(blocks):
        slot = prefix[b : b + 1] + offset
        hit = (slot == rank) & (mine[b : b + 1] > 0.0)
        where += jnp.sum(
            jnp.where(hit, local_ref[b : b + 1, :].astype(F32) + 1.0, 0.0), axis=1, keepdims=True
        )
        offset = offset + totals[b : b + 1]
    positions = lax.broadcasted_iota(jnp.int32, (padded, rows), 1).astype(F32)
    onehot = jnp.where(where == positions, 1.0, 0.0).astype(BF16)
    points = nn(onehot, emb_ref[...])
    high, low = split(fac_ref[...])
    picked = nn(onehot, high) + nn(onehot, low)
    start = 0
    for out_ref in out_refs:
        size = out_ref.shape[0]
        out_ref[:, :width] = points[start : start + size]
        out_ref[:, width:] = picked[start : start + size]
        start += size


def main_kernel(
    width,
    blocks,
    idx_ref,
    emb_ref,
    fac_ref,
    diag_ref,
    *refs,
):
    nbuf = len(refs) - 2 - 12
    buf_refs = refs[:nbuf]
    out_ref, newdiag_ref = refs[nbuf : nbuf + 2]
    stage, gathered, e_ref, fh_ref, fl_ref, sq_ref, rg, w_ref, wh_ref, wl_ref, sums, sem = refs[nbuf + 2 :]
    local = emb_ref.shape[0]
    total = idx_ref.shape[0]
    k = total // blocks
    rank = fac_ref.shape[1]
    copies = []
    start = 0
    for i, buf in enumerate(buf_refs):
        copies.append(
            pltpu.make_async_copy(buf, stage.at[pl.ds(start, buf.shape[0]), :], sem.at[i])
        )
        start += buf.shape[0]
    for copy in copies:
        copy.start()
    e_ref[total:, :] = emb_ref[...]
    high, low = split(fac_ref[...])
    fh_ref[total:, :rank] = high
    fl_ref[total:, :rank] = low
    wide = emb_ref[...].astype(F32)
    sq_ref[total:, :] = jnp.sum(wide * wide, axis=1, keepdims=True)
    for copy in copies:
        copy.wait()

    row_squares = [None] * blocks

    def gather(b, unrolled):
        def some(g, carry):
            for j in range(8):
                at = b * k + g * 8 + j
                gathered[pl.ds(at, 1), :] = stage[pl.ds(idx_ref[at], 1), :]
            return carry

        if unrolled:
            for g in range(k // 8):
                some(g, 0)
        else:
            lax.fori_loop(0, k // 8, some, 0)

    def prepare(b):
        rows = pl.ds(b * k, k)
        wide = gathered[rows, :width]
        e_ref[rows, :] = wide.astype(BF16)
        high, low = split(gathered[rows, width:])
        fh_ref[rows, :rank] = high
        fl_ref[rows, :rank] = low
        square = wide * wide
        sq_ref[rows, :] = jnp.sum(square, axis=1, keepdims=True)
        row_squares[b] = row_sums(square)

    unroll = True
    gather(0, False)
    if not unroll:
        for b in range(1, blocks):
            gather(b, False)
    prepare(0)
    tiles = (total + local) // k

    def tile(t, stop, b, known):
        cols = pl.ds(b * k, k)
        rows = pl.ds(t * k, (stop - t) * k)
        depth = rank + known * k
        inner = nt(e_ref[rows, :], e_ref[cols, :])
        kernel = jnp.exp(-gamma_scale * (sq_ref[rows, :] + row_squares[b] - 2.0 * inner))
        left = fh_ref[rows, :depth], fl_ref[rows, :depth]
        right = fh_ref[cols, :depth], fl_ref[cols, :depth]
        rg[rows, b * k : (b + 1) * k] = kernel - nt3(left, right)

    def columns(t, stop, b):
        rows = pl.ds(t * k, (stop - t) * k)
        new = nt3(split(rg[rows, b * k : (b + 1) * k]), (wh_ref[b], wl_ref[b]))
        if stop == tiles:
            mine = new[new.shape[0] - local :]
            out_ref[:, b * k : (b + 1) * k] = mine
            sums[b] = row_sums(mine * mine)
        if b + 1 < blocks:
            high, low = split(new)
            fh_ref[rows, rank + b * k : rank + (b + 1) * k] = high
            fl_ref[rows, rank + b * k : rank + (b + 1) * k] = low
            return high, low

    row = lax.broadcasted_iota(jnp.int32, (k, k), 0)
    col = lax.broadcasted_iota(jnp.int32, (k, k), 1)
    identity = jnp.where(row == col, 1.0, 0.0)
    lower = jnp.where(row > col, 1.0, 0.0) + 0.5 * identity
    tile(0, 1, 0, 0)
    for b in range(blocks):
        ahead = []
        if b == 0:
            ahead.append(functools.partial(gather, 1, True))
            ahead.append(functools.partial(tile, blocks, blocks + 1, 0, 0))
            ahead.append(functools.partial(prepare, 1))
            ahead.append(functools.partial(gather, 2, True))
            ahead.append(functools.partial(tile, blocks + 1, tiles, 0, 0))
            ahead.append(functools.partial(prepare, 2))
            ahead.append(functools.partial(gather, 3, True))
            ahead.append(functools.partial(tile, 1, 2, 0, 0))
            ahead.append(functools.partial(prepare, 3))
            ahead.append(functools.partial(tile, 1, 2, 1, 0))
            ahead.append(functools.partial(tile, 2, blocks, 0, 0))
        else:
            ahead.append(functools.partial(columns, b + 1, tiles, b - 1))
            if b + 1 < blocks:
                ahead.append(functools.partial(tile, b + 1, b + 2, b + 1, b))
            middle = (b + 1 + tiles) // 2
            ahead.append(functools.partial(tile, b + 1, middle, b, b))
            ahead.append(functools.partial(tile, middle, tiles, b, b))
        quarter = -(-len(ahead) // 4)

        def filler(ahead=ahead, quarter=quarter):
            for _ in range(min(quarter, len(ahead))):
                ahead.pop(0)()

        gram = rg[b * k : (b + 1) * k, b * k : (b + 1) * k]
        diag = jnp.sum(gram * identity, axis=0, keepdims=True)
        off = jnp.sum(jnp.abs(gram), axis=0, keepdims=True) - jnp.abs(diag)
        shift = ridge_base + jnp.maximum(jnp.max(off - diag, axis=1, keepdims=True), 0.0)
        scale = SPREAD * (shift + jnp.max(diag, axis=1, keepdims=True))
        shifted = (gram + shift * identity) / scale
        sh, sl = split(shifted)

        def update(error):
            f = error * lower
            fb = f.astype(BF16)
            return f - nn(fb, fb) - nt(fb, fb) * lower

        def newton(away, fill):
            ws = split(identity - away)
            product = split(nn3(ws, (sh, sl)))
            fill()
            error = nt3(product, ws) - identity
            fill()
            step = update(error)
            fill()
            moved = step - nn(step.astype(BF16), away.astype(BF16))
            eb = error.astype(BF16)
            twice = nt(eb, eb)
            return away + moved, jnp.sum(twice * twice)

        away = update(shifted - identity)
        filler()
        away, norm = newton(away, filler)
        while ahead:
            filler()
        w_ref[...] = away

        def more(state):
            i, norm = state
            return jnp.logical_and(i < MAX_NEWTON, jnp.logical_not(norm < TOL4))

        def again(state):
            i, norm = state
            away, norm = newton(w_ref[...], lambda: None)
            w_ref[...] = away
            return i + 1, norm

        _, norm = lax.while_loop(more, again, (0, norm))
        w_ref[...] = identity - w_ref[...]

        @pl.when(jnp.logical_not(norm < TOL4))
        def _():
            left = rg.at[b * k : (b + 1) * k, b * k : (b + 1) * k]
            left[...] = shifted
            w_ref[...] = identity

            def eliminate(j, carry):
                pivot_row = left[pl.ds(j, 1), :]
                unit_row = w_ref[pl.ds(j, 1), :]
                at = lax.broadcasted_iota(jnp.int32, (1, k), 1) == j
                pivot = jnp.sum(jnp.where(at, pivot_row, 0.0), axis=1, keepdims=True)
                column = jnp.sum(jnp.where(at, left[...], 0.0), axis=1, keepdims=True)
                below = lax.broadcasted_iota(jnp.int32, (k, 1), 0) > j
                times = jnp.where(below, column / pivot, 0.0)
                left[...] = left[...] - times * pivot_row
                w_ref[...] = w_ref[...] - times * unit_row
                w_ref[pl.ds(j, 1), :] = unit_row * lax.rsqrt(pivot)
                return carry

            lax.fori_loop(0, k, eliminate, 0)

        wh_ref[b], wl_ref[b] = split(w_ref[...] * lax.rsqrt(scale))
        if b + 1 < blocks:
            new = columns(b + 1, b + 2, b)
            at = slice((b + 1) * k, (b + 2) * k)
            rg[at, at] -= nt3(new, new)
        else:
            columns(b + 1, tiles, b)
    newdiag_ref[...] = diag_ref[...] - functools.reduce(jnp.add, [sums[b] for b in range(blocks)])


def on_device(n, base, spare, sizes, orders, embeddings, factor, diagonal, pivot_owner, pivot_local):
    rows, width = embeddings.shape
    rank = factor.shape[1]
    blocks, pivots = pivot_owner.shape
    total = blocks * pivots
    device = lax.axis_index("rows") * lax.axis_size("sub") + lax.axis_index("sub")
    cap = sum(sizes)
    vmem = pl.BlockSpec(memory_space=pltpu.VMEM)
    smem = pl.BlockSpec(memory_space=pltpu.SMEM)
    anywhere = pl.BlockSpec(memory_space=pl.ANY)
    *parts, give = pl.pallas_call(
        functools.partial(select_kernel, sizes),
        name="select_pivots",
        out_shape=[jax.ShapeDtypeStruct((size, width + rank), F32) for size in sizes + [spare]],
        in_specs=[smem, vmem, vmem, vmem, vmem],
        out_specs=[vmem] * (len(sizes) + 1),
    )(device.reshape(1), pivot_owner, pivot_local, embeddings, factor)

    def flip(bit, x):
        return lax.ppermute(x, AXES, [(d, d ^ (1 << bit)) for d in range(n)])

    parts[-1] = parts[-1] + flip(0, give)
    last = len(orders[0]) - 1
    for stage in range(last):
        for p, order in enumerate(orders):
            parts[p] = jnp.concatenate([parts[p], flip(order[stage], parts[p])], axis=0)
    buffers = []
    for part, order in zip(parts, orders, strict=True):
        buffers += [part, flip(order[last], part)]
    buffers += [flip(0, buffer) for buffer in buffers]

    owner = pivot_owner.reshape(-1)
    order_of = jnp.arange(total)
    same = owner[:, None] == owner[None, :]
    slot = jnp.sum((same & (order_of[None, :] < order_of[:, None])).astype(jnp.int32), axis=1)
    others = jnp.sum((owner[:, None] == (owner[None, :] ^ 1)).astype(jnp.int32), axis=1)
    shared = slot - base + (owner & 1) * jnp.maximum(others - base, 0)
    spilled = slot >= base
    overflow = jnp.max(jnp.where(spilled, shared, 0)) >= 2 * spare
    holder = jnp.where(spilled, (owner & ~1) | jnp.clip(shared // spare, 0, 1), owner)
    slot = jnp.where(spilled, base + shared % spare, slot)
    relative = holder ^ device
    half = n // 2
    idx = jnp.zeros_like(slot)
    start, begin = 0, 0
    for size, order in zip(sizes, orders, strict=True):
        place = jnp.zeros_like(slot)
        for i, bit in enumerate(order):
            place += ((relative >> bit) & 1) << i
        at = begin + place * size + (slot - start)
        here = (slot >= start) & (slot < start + size)
        idx = jnp.where(here, at + (relative & 1) * (half * cap), idx)
        start += size
        begin += half * size

    def run_blocks(idx, buffers):
        k = pivots
        return pl.pallas_call(
            functools.partial(main_kernel, width, blocks),
            name="pivot_blocks",
            out_shape=[
                jax.ShapeDtypeStruct((rows, total), F32),
                jax.ShapeDtypeStruct((1, rows), F32),
            ],
            in_specs=[smem, vmem, vmem, vmem] + [anywhere] * len(buffers),
            out_specs=[vmem, vmem],
            scratch_shapes=[
                pltpu.VMEM((n * cap, width + rank), F32),
                pltpu.VMEM((total, width + rank), F32),
                pltpu.VMEM((total + rows, width), BF16),
                pltpu.VMEM((total + rows, rank + total - k), BF16),
                pltpu.VMEM((total + rows, rank + total - k), BF16),
                pltpu.VMEM((total + rows, 1), F32),
                pltpu.VMEM((total + rows, total), F32),
                pltpu.VMEM((k, k), F32),
                pltpu.VMEM((blocks, k, k), BF16),
                pltpu.VMEM((blocks, k, k), BF16),
                pltpu.VMEM((blocks, 1, rows), F32),
                pltpu.SemaphoreType.DMA((len(buffers),)),
            ],
            compiler_params=pltpu.CompilerParams(vmem_limit_bytes=n * cap * (width + rank) * 4 + 36 * 1024 * 1024),
        )(idx, embeddings, factor, diagonal.reshape(1, rows), *buffers)

    def slow(idx, *buffers):
        positions = lax.broadcasted_iota(jnp.int32, (total, rows), 1)
        hits = (owner[:, None] == device) & (pivot_local.reshape(-1)[:, None] == positions)
        hits = hits.astype(F32)
        points = jnp.dot(hits.astype(BF16), embeddings, preferred_element_type=F32)
        picked = jnp.dot(hits, factor, precision=lax.Precision.HIGHEST)
        everything = jnp.concatenate([points, picked], axis=1)
        for bit in range(n.bit_length() - 1):
            everything = everything + flip(bit, everything)
        everything = jnp.pad(everything, ((0, max(0, n * cap - total)), (0, 0)))
        pieces, start = [], 0
        for buffer in buffers:
            pieces.append(everything[start : start + buffer.shape[0]])
            start += buffer.shape[0]
        return jnp.arange(total, dtype=jnp.int32), *pieces

    idx, *buffers = lax.cond(overflow, slow, lambda *held: held, idx, *buffers)
    new_columns, new_diagonal = run_blocks(idx, buffers)
    return new_columns, new_diagonal.reshape(rows)


def solution(mesh):
    n = mesh.shape["rows"] * mesh.shape["sub"]

    def program(embeddings, factor, diagonal, pivot_owner, pivot_local):
        base, spare, sizes, orders = plan(n, pivot_owner.size)
        spec = P(AXES)
        return jax.shard_map(
            functools.partial(on_device, n, base, spare, sizes, orders),
            mesh=mesh,
            in_specs=(P(AXES, None), P(AXES, None), spec, P(), P()),
            out_specs=(P(AXES, None), spec),
            check_vma=False,
        )(embeddings, factor, diagonal, pivot_owner, pivot_local)

    return program
```
